32 devices in a mesh: gx: 4 (over z), gy: 4 (over x, core), gz: 2 (over y).
Axes of the slice: x: 2, y: 2, z: 4, core: 2. Of those that a mesh axis runs over, the one named last changes fastest.
Arguments:
- activations: bfloat16 [1024, 8192], P('gy', 'gx'), may hold values from -0.5 to 0.5
- cotangent: bfloat16 [1024, 8192], P('gy', 'gx'), may hold values from -1.5 to 1.5
- gate_pre: bfloat16 [1024, 26624], P('gx', ('gy', 'gz')), may hold values from -6 to 6
- up_pre: bfloat16 [1024, 26624], P('gx', ('gy', 'gz')), may hold values from -6 to 6
- gate_weight: bfloat16 [8192, 26624], P('gx', ('gy', 'gz')), may hold values from -0.0625 to 0.0625
- up_weight: bfloat16 [8192, 26624], P('gx', ('gy', 'gz')), may hold values from -0.0625 to 0.0625
- down_weight: bfloat16 [26624, 8192], P(('gy', 'gz'), 'gx'), may hold values from -0.15625 to 0.15625
Outputs:
- input_grad: bfloat16 [1024, 8192], P('gy', 'gx')
- gate_grad: bfloat16 [8192, 26624], P('gx', ('gy', 'gz'))
- up_grad: bfloat16 [8192, 26624], P('gx', ('gy', 'gz'))
- down_grad: bfloat16 [26624, 8192], P(('gy', 'gz'), 'gx')
The draws below stay inside these ranges and needn't reach their ends.
All inputs are finite; a program needn't handle non-finite values.
Results may differ from the reference program's by a relative error of at most 0.015.
Values may be sent and summed in bfloat16 or wider, within the bound.
A program may use at most 192 MiB of HBM per device.

```python
import jax
import jax.numpy as jnp
from jax import lax

D = 8192
F = 26624
TOKENS = 1024


def steps_of(own_key, dims, split, least, largest):
    def one(axis_at, parts):
        steps = jax.random.uniform(jax.random.fold_in(jax.random.fold_in(own_key, 6), axis_at), (parts,), jnp.float32, least / len(split), largest / len(split))
        return jnp.repeat(jnp.exp(steps), dims[axis_at] // parts).reshape((-1,) + (1,) * (len(dims) - axis_at - 1))

    level = one(*split[0])
    for cut in split[1:]:
        level = level * one(*cut)
    return level


def centred(own_key, extent, scale, limit, shards=(), held_as=jnp.bfloat16):
    drawn = scale * jax.random.normal(own_key, extent, jnp.float32)
    if shards:
        drawn = drawn * steps_of(own_key, extent, shards, -0.22, 0.18)
    return jnp.clip(drawn, -limit, limit).astype(held_as)


def setup_inputs(seed: int = 0) -> dict:
    streams_of = jax.random.split(jax.random.key(seed), 8)
    activations = centred(streams_of[0], (TOKENS, D), 0.08, 0.5, ((0, 4), (1, 4)))
    cotangent = centred(streams_of[1], (TOKENS, D), 0.25, 1.5, ((0, 4), (1, 4)))
    gate_pre = centred(streams_of[2], (TOKENS, F), 1.0, 6.0, ((0, 4), (1, 8)))
    up_pre = centred(streams_of[3], (TOKENS, F), 1.0, 6.0, ((0, 4), (1, 8)))
    gate_weight = centred(streams_of[4], (D, F), D ** -0.5, 0.0625, ((0, 4), (1, 8)))
    up_weight = centred(streams_of[5], (D, F), D ** -0.5, 0.0625, ((0, 4), (1, 8)))
    down_weight = centred(streams_of[6], (F, D), (F // 16) ** -0.5, 0.15625, ((0, 8), (1, 4)))
    return dict(activations=activations, cotangent=cotangent, gate_pre=gate_pre, up_pre=up_pre, gate_weight=gate_weight, up_weight=up_weight, down_weight=down_weight)


def swiglu_grads(gate_in, up_in, grad_hidden):
    gate_val = gate_in.astype(jnp.float32)
    up_val = up_in.astype(jnp.float32)
    sigmoid = jax.nn.sigmoid(gate_val)
    hidden = (gate_val * sigmoid * up_val).astype(jnp.bfloat16)
    grad_gate = (grad_hidden * up_val * sigmoid * (1.0 + gate_val * (1.0 - sigmoid))).astype(jnp.bfloat16)
    grad_up = (grad_hidden * gate_val * sigmoid).astype(jnp.bfloat16)
    return hidden, grad_gate, grad_up


def reference(activations, cotangent, gate_pre, up_pre, gate_weight, up_weight, down_weight):
    over_rows = (((0,), (0,)), ((), ()))
    over_cols = (((1,), (1,)), ((), ()))
    grad_hidden = lax.dot_general(cotangent, down_weight, over_cols, preferred_element_type=jnp.float32)
    hidden, grad_gate, grad_up = swiglu_grads(gate_pre, up_pre, grad_hidden)
    down_grad = lax.dot_general(hidden, cotangent, over_rows, preferred_element_type=jnp.float32).astype(jnp.bfloat16)
    gate_grad = lax.dot_general(activations, grad_gate, over_rows, preferred_element_type=jnp.float32).astype(jnp.bfloat16)
    up_grad = lax.dot_general(activations, grad_up, over_rows, preferred_element_type=jnp.float32).astype(jnp.bfloat16)
    input_grad = lax.dot_general(grad_gate, gate_weight, over_cols, preferred_element_type=jnp.float32)
    input_grad = input_grad + lax.dot_general(grad_up, up_weight, over_cols, preferred_element_type=jnp.float32)
    return input_grad.astype(jnp.bfloat16), gate_grad, up_grad, down_grad
```

```python
import jax
import jax.numpy as jnp
from jax import lax
from jax.sharding import PartitionSpec as P

over_rows = (((0,), (0,)), ((), ()))
over_cols = (((1,), (1,)), ((), ()))
BF = jnp.bfloat16
F32 = jnp.float32


def swiglu_grads(gate_in, up_in, grad_hidden):
    gate_val = gate_in.astype(F32)
    up_val = up_in.astype(F32)
    grad_hidden = grad_hidden.astype(F32)
    sigmoid = jax.nn.sigmoid(gate_val)
    hidden = (gate_val * sigmoid * up_val).astype(BF)
    grad_gate = (grad_hidden * up_val * sigmoid * (1.0 + gate_val * (1.0 - sigmoid))).astype(BF)
    grad_up = (grad_hidden * gate_val * sigmoid).astype(BF)
    return hidden, grad_gate, grad_up


def after(value, earlier):
    seen = earlier.reshape(-1)[0].astype(F32)
    return value + jnp.minimum(jnp.abs(seen), 0.0).astype(value.dtype)


def line_gather(block, axis, n):
    me = lax.axis_index(axis)
    right, left = {}, {}
    from_left = from_right = block
    for s in range(1, n):
        from_left = lax.ppermute(from_left, axis, [(i, i + 1) for i in range(s - 1, n - 1)])
        from_right = lax.ppermute(from_right, axis, [(i, i - 1) for i in range(1, n - s + 1)])
        right[s], left[s] = from_left, from_right
    return [block] + [jnp.where(me >= r, right[r], left[n - r]) for r in range(1, n)]


def line_scatter(part, axis, n):
    right = left = None
    for t in range(1, n):
        to_right, to_left = part(n - t), part(t)
        if right is not None:
            to_right = to_right + right.astype(F32)
            to_left = to_left + left.astype(F32)
        right = lax.ppermute(
            to_right.astype(BF), axis, [(i, i + 1) for i in range(min(t, n - 1))]
        )
        left = lax.ppermute(
            to_left.astype(BF), axis, [(i, i - 1) for i in range(max(n - t, 1), n)]
        )
    total = part(0)
    if right is not None:
        total = total + right.astype(F32) + left.astype(F32)
    return total


def pair_scatter(total, axis, n):
    me = lax.axis_index(axis)
    if n & (n - 1):
        return lax.psum_scatter(total, axis, scatter_dimension=0, tiled=False)
    stride = 1
    while stride < n:
        pairs = total.reshape((total.shape[0] // 2, 2) + total.shape[1:])
        bit = (me // stride) % 2
        mine = lax.dynamic_index_in_dim(pairs, bit, 1, keepdims=False)
        theirs = lax.dynamic_index_in_dim(pairs, 1 - bit, 1, keepdims=False)
        got = lax.ppermute(theirs.astype(BF), axis, [(i, i ^ stride) for i in range(n)])
        total = mine + got.astype(F32)
        stride *= 2
    return total[0]


def chunks_of(width):
    tile = 256 if width % 256 == 0 else 64
    units = width // tile
    if width < 2048:
        return [(0, width)]
    sizes = [(units * 5 + 6) // 13, (units * 5 + 6) // 13]
    sizes.append(units - sum(sizes))
    out, at = [], 0
    for size in sizes:
        out.append((at * tile, size * tile))
        at += size
    return out


def shards(activations, cotangent, gate_pre, up_pre, gate_weight, up_weight, down_weight):
    n, ny, nz = lax.axis_size("gx"), lax.axis_size("gy"), lax.axis_size("gz")
    me = lax.axis_index("gx")
    rows = gate_pre.shape[0]
    tokens = n * rows
    width = gate_pre.shape[1]
    feats = activations.shape[1]
    cotangent_all = lax.all_gather(cotangent, "gy", axis=0, tiled=True)
    activations_all = lax.all_gather(activations, "gy", axis=0, tiled=True)

    def relative(whole):
        blocks = whole.reshape(n, rows, whole.shape[1])
        return jnp.concatenate(
            [
                lax.dynamic_index_in_dim(blocks, lax.rem(me - r + n, n), 0, keepdims=False)
                for r in range(n)
            ],
            axis=0,
        )

    cot = relative(cotangent_all)
    act = relative(activations_all)
    total = None
    gate_grad = jnp.zeros((feats, width), BF)
    up_grad = jnp.zeros((feats, width), BF)
    down_grad = jnp.zeros((width, feats), BF)
    chunks = chunks_of(width)
    partials = [
        lax.dot_general(
            cot, lax.slice_in_dim(down_weight, at, at + size, axis=0), over_cols,
            preferred_element_type=F32,
        ).reshape(n, rows, size)
        for at, size in chunks
    ]
    gates, sums = [], []
    for k, (at, size) in enumerate(chunks):
        gate = lax.slice_in_dim(gate_pre, at, at + size, axis=1)
        up = lax.slice_in_dim(up_pre, at, at + size, axis=1)
        if k == 1:
            gate, up = after(gate, partials[1]), after(up, partials[1])
        if k >= 2:
            gate, up = after(gate, sums[k - 2]), after(up, sums[k - 2])
        gates.append((line_gather(gate, "gx", n), line_gather(up, "gx", n)))

        def part(r, k=k):
            term = partials[k][(n - r) % n]
            return after(term, sums[k - 1]) if k and r in (1, n - 1) else term

        sums.append(line_scatter(part, "gx", n).astype(BF))
    for (at, size), (gate, up), own in zip(chunks, gates, sums):
        grad_hidden = line_gather(own, "gx", n)
        done = [swiglu_grads(*terms) for terms in zip(gate, up, grad_hidden)]
        hidden, grad_gate, grad_up = (jnp.concatenate(part, axis=0) for part in zip(*done))
        term = lax.dot_general(
            grad_gate, lax.slice_in_dim(gate_weight, at, at + size, axis=1), over_cols,
            preferred_element_type=F32,
        ) + lax.dot_general(
            grad_up, lax.slice_in_dim(up_weight, at, at + size, axis=1), over_cols,
            preferred_element_type=F32,
        )
        total = term if total is None else total + term
        down = lax.dot_general(hidden, cot, over_rows, preferred_element_type=F32).astype(BF)
        first = lax.dot_general(act, grad_gate, over_rows, preferred_element_type=F32).astype(BF)
        second = lax.dot_general(act, grad_up, over_rows, preferred_element_type=F32).astype(BF)
        down_grad = lax.dynamic_update_slice(down_grad, down, (at, 0))
        gate_grad = lax.dynamic_update_slice(gate_grad, first, (0, at))
        up_grad = lax.dynamic_update_slice(up_grad, second, (0, at))
    total = total.reshape(n, rows, feats)
    total = jnp.stack(
        [lax.dynamic_index_in_dim(total, lax.rem(me - j + n, n), 0, keepdims=False) for j in range(n)]
    ).reshape(ny, tokens // ny, feats)
    share = pair_scatter(total, "gy", ny)
    if nz == 2:
        share = share + lax.ppermute(share.astype(BF), "gz", [(0, 1), (1, 0)]).astype(F32)
        input_grad = share.astype(BF)
    else:
        input_grad = lax.psum(share, "gz").astype(BF)
    return input_grad, gate_grad, up_grad, down_grad


def solution(mesh):
    in_specs = (
        P("gy", "gx"),
        P("gy", "gx"),
        P("gx", ("gy", "gz")),
        P("gx", ("gy", "gz")),
        P("gx", ("gy", "gz")),
        P("gx", ("gy", "gz")),
        P(("gy", "gz"), "gx"),
    )
    out_specs = (P("gy", "gx"), P("gx", ("gy", "gz")), P("gx", ("gy", "gz")), P(("gy", "gz"), "gx"))
    return jax.shard_map(shards, mesh=mesh, in_specs=in_specs, out_specs=out_specs, check_vma=False)
```
